32 devices in a mesh: ens: 2 (over y), hist: 4 (over z), mom: 2 (over x), rep: 2 (over core).
Axes of the slice: x: 2, y: 2, z: 4, core: 2. Of those that a mesh axis runs over, the one named last changes fastest.
Arguments:
- history_stat: float32 [512, 1024, 512], P(('hist', 'rep'), 'ens', 'mom'), parts along dimension 1, may hold values from -6 to 6, as said below
- history_spec: float32 [512, 1024, 512], P(('hist', 'rep'), 'ens', 'mom'), parts along dimension 1, may hold values from -6 to 6, as said below
Outputs:
- rows_stat: float32 [6, 512, 512], P('ens', ('hist', 'rep'), 'mom'), parts along dimension 0
- rows_spec: float32 [6, 512, 512], P('ens', ('hist', 'rep'), 'mom'), parts along dimension 0
- newest_stat: float32 [10, 5, 512], P('ens', None, 'mom'), parts along dimension 0
- newest_spec: float32 [10, 5, 512], P('ens', None, 'mom'), parts along dimension 0
The draws below stay inside these ranges and needn't reach their ends.
There are 2 independent parts, one for each index of `ens`. The reference program is written for one: setup_inputs(seed, part) draws one part's arguments, and reference() takes and returns one part's arrays. A program takes and returns all parts, laid end to end along the dimension named above; each array names one. Nothing has to cross between parts.
Inputs may be any that keep to these rules, and one draw needn't show every extreme that they name: `history_stat`: symmetric under exchange of its two time indices. `history_spec`: antisymmetric under exchange of its two time indices, zero where they are equal.
All inputs are finite; a program needn't handle non-finite values.
Results may differ from the reference program's by a relative error of at most 0.0003.
Values sent between devices are 32-bit elements; how exact they have to be, the bound alone decides.
A program may use at most 128 MiB of HBM per device.

```python
import math
import jax
import jax.numpy as jnp
from jax import lax

TIMES = 512
MOMENTA = 512
STEPS = 3


def clipped_base(key, salt):
    base = jax.random.normal(jax.random.fold_in(key, salt), (TIMES, TIMES, MOMENTA), jnp.float32)
    return jnp.clip(base, -6.0, 6.0)


def draw_history_stat(key, part):
    base = clipped_base(key, 11)
    field = 0.5 * (base + jnp.transpose(base, (1, 0, 2)))
    return field


def draw_history_spec(key, part):
    base = clipped_base(key, 17)
    field = 0.5 * (base - jnp.transpose(base, (1, 0, 2)))
    return field


def setup_inputs(seed: int = 0, part: int = 0) -> dict:
    key_list = jax.random.split(jax.random.key(seed), 3)
    own_keys = jax.random.split(jax.random.fold_in(key_list[2], part), 3)
    history_stat = draw_history_stat(jax.random.fold_in(jax.random.fold_in(key_list[2], part), 71), part)
    history_spec = draw_history_spec(jax.random.fold_in(jax.random.fold_in(key_list[2], part), 71), part)
    return dict(history_stat=history_stat, history_spec=history_spec)


TIME_STEP = 0.12
CUTOFF = 12.8
MASS_SQUARED = 1.0
SUNSET_COUPLING = 100.0
HARTREE_COUPLING = 2.45
HIGHEST = lax.Precision.HIGHEST


def sine_values(left_index, right_index, points):
    product = ((left_index[:, None] + 1) * (right_index[None, :] + 1)) % (2 * (points + 1))
    return jnp.sin(product.astype(jnp.float32) * (math.pi / (points + 1)))


def forward_table(momentum_index, radius_index, points):
    momentum_step = CUTOFF / points
    radius_step = math.pi / ((points + 1) * momentum_step)
    momentum = (momentum_index.astype(jnp.float32) + 1.0) * momentum_step
    radius = (radius_index.astype(jnp.float32) + 1.0) * radius_step
    return sine_values(momentum_index, radius_index, points) * (momentum[:, None] * momentum_step) / (2.0 * math.pi ** 2 * radius[None, :])


def backward_table(radius_index, momentum_index, points):
    momentum_step = CUTOFF / points
    radius_step = math.pi / ((points + 1) * momentum_step)
    momentum = (momentum_index.astype(jnp.float32) + 1.0) * momentum_step
    radius = (radius_index.astype(jnp.float32) + 1.0) * radius_step
    return sine_values(radius_index, momentum_index, points) * (4.0 * math.pi * radius_step * radius[:, None]) / momentum[None, :]


def sunset(field_stat, field_spec):
    square_stat = field_stat * field_stat
    square_spec = field_spec * field_spec
    sigma_stat = -SUNSET_COUPLING * field_stat * (square_stat - 0.75 * square_spec)
    sigma_spec = -SUNSET_COUPLING * field_spec * (3.0 * square_stat - 0.25 * square_spec)
    return sigma_stat, sigma_spec


def reference(history_stat, history_spec):
    time_count = TIMES
    row_count = TIMES
    newest = STEPS + 2
    momentum_step = CUTOFF / MOMENTA
    row_times = jnp.arange(row_count, dtype=jnp.int32)
    column_times = jnp.arange(time_count, dtype=jnp.int32)
    newest_times = time_count - 2 + jnp.arange(newest, dtype=jnp.int32)
    newest_index = jnp.arange(newest, dtype=jnp.int32)
    later_mask = (row_times[:, None] <= column_times[None, :]).astype(jnp.float32)
    earlier_mask = (row_times[:, None] >= column_times[None, :]).astype(jnp.float32)
    newest_later = (row_times[:, None] <= newest_times[None, :]).astype(jnp.float32)
    newest_earlier = (row_times[:, None] >= newest_times[None, :]).astype(jnp.float32)
    upper_pairs = (newest_index[:, None] <= newest_index[None, :]).astype(jnp.float32)
    lower_pairs = (newest_index[:, None] >= newest_index[None, :]).astype(jnp.float32)
    every_index = jnp.arange(MOMENTA, dtype=jnp.int32)
    momentum = (every_index.astype(jnp.float32) + 1.0) * momentum_step
    measure = momentum * momentum * momentum_step / (2.0 * math.pi ** 2)
    forward = forward_table(every_index, every_index, MOMENTA)
    backward = backward_table(every_index, every_index, MOMENTA)
    block_stat = jnp.zeros((newest, newest, MOMENTA), jnp.float32).at[:2, :2].set(history_stat[time_count - 2:, time_count - 2:, :])
    block_spec = jnp.zeros((newest, newest, MOMENTA), jnp.float32).at[:2, :2].set(history_spec[time_count - 2:, time_count - 2:, :])
    column_stat = jnp.zeros((newest, row_count, MOMENTA), jnp.float32).at[:2].set(jnp.transpose(history_stat[:, time_count - 2:, :], (1, 0, 2)))
    column_spec = jnp.zeros((newest, row_count, MOMENTA), jnp.float32).at[:2].set(-jnp.transpose(history_spec[:, time_count - 2:, :], (1, 0, 2)))
    factor = TIME_STEP * TIME_STEP
    for step_index in range(STEPS):
        current = step_index + 1
        stack_stat = jnp.concatenate([column_stat[current], block_stat[current]], axis=0)
        stack_spec = jnp.concatenate([column_spec[current], block_spec[current]], axis=0)
        tadpole = jnp.sum(measure * block_stat[current, current])
        radial_stat = jnp.dot(stack_stat, forward, precision=HIGHEST)
        radial_spec = jnp.dot(stack_spec, forward, precision=HIGHEST)
        sigma_stat, sigma_spec = sunset(radial_stat, radial_spec)
        sigma_stat = jnp.dot(sigma_stat, backward, precision=HIGHEST)
        sigma_spec = jnp.dot(sigma_spec, backward, precision=HIGHEST)
        group_stat, newest_sstat = sigma_stat[:row_count], sigma_stat[row_count:]
        group_spec, newest_sspec = sigma_spec[:row_count], sigma_spec[row_count:]
        memory_stat = jnp.einsum("ip,it,itp->tp", group_stat, later_mask, history_spec, precision=HIGHEST) - jnp.einsum("ip,itp->tp", group_spec, history_stat, precision=HIGHEST)
        memory_spec = -jnp.einsum("ip,it,itp->tp", group_spec, earlier_mask, history_spec, precision=HIGHEST)
        newest_mstat = -jnp.einsum("ip,aip->ap", group_spec, column_stat, precision=HIGHEST) - jnp.einsum("ip,ia,aip->ap", group_stat, newest_later, column_spec, precision=HIGHEST)
        newest_mspec = jnp.einsum("ip,ia,aip->ap", group_spec, newest_earlier, column_spec, precision=HIGHEST)
        active = ((newest_index >= 2) & (newest_index <= current)).astype(jnp.float32)[:, None]
        weight_spec = newest_sspec * active
        weight_stat = newest_sstat * active
        memory_stat = memory_stat - jnp.einsum("bp,bip->ip", weight_spec, column_stat, precision=HIGHEST)
        memory_spec = memory_spec - jnp.einsum("bp,bip->ip", weight_spec, column_spec, precision=HIGHEST)
        newest_mstat = newest_mstat - jnp.einsum("bp,bap->ap", weight_spec, block_stat, precision=HIGHEST) + jnp.einsum("bp,ba,bap->ap", weight_stat, upper_pairs, block_spec, precision=HIGHEST)
        newest_mspec = newest_mspec - jnp.einsum("bp,ba,bap->ap", weight_spec, lower_pairs, block_spec, precision=HIGHEST)
        frequency = momentum * momentum + MASS_SQUARED + HARTREE_COUPLING * tadpole
        next_stat = 2.0 * column_stat[current] - column_stat[step_index] - factor * (frequency * column_stat[current] + TIME_STEP * memory_stat)
        next_spec = 2.0 * column_spec[current] - column_spec[step_index] - factor * (frequency * column_spec[current] + TIME_STEP * memory_spec)
        column_stat = column_stat.at[current + 1].set(next_stat)
        column_spec = column_spec.at[current + 1].set(next_spec)
        valid_mask = (newest_index <= current).astype(jnp.float32)[:, None]
        line_stat = valid_mask * (2.0 * block_stat[current] - block_stat[step_index] - factor * (frequency * block_stat[current] + TIME_STEP * newest_mstat))
        line_spec = valid_mask * (2.0 * block_spec[current] - block_spec[step_index] - factor * (frequency * block_spec[current] + TIME_STEP * newest_mspec))
        diagonal = 2.0 * line_stat[current] - line_stat[step_index] - factor * (frequency * line_stat[current] + TIME_STEP * newest_mstat[current])
        line_stat = line_stat.at[current + 1].set(diagonal)
        block_stat = block_stat.at[current + 1].set(line_stat).at[:, current + 1].set(line_stat)
        block_spec = block_spec.at[current + 1].set(line_spec).at[:, current + 1].set(-line_spec)
    return column_stat[2:], column_spec[2:], block_stat, block_spec
```

```python
import functools
import math

import jax
import jax.numpy as jnp
import ml_dtypes
import numpy as np
from jax import lax
from jax.experimental import pallas as pl
from jax.experimental.pallas import tpu as pltpu
from jax.sharding import PartitionSpec as P

STEPS = 3
TIME_STEP = 0.12
CUTOFF = 12.8
MASS_SQUARED = 1.0
SUNSET_COUPLING = 100.0
HARTREE_COUPLING = 2.45
MESH = pl.DeviceIdType.MESH
LANES = 128
TILE = 8
ROWS_AT_ONCE = 4
SLOTS = 3
RESIDENT_BYTES = 48 << 20
F32 = jnp.float32
BF16 = jnp.bfloat16


def sine_table(points):
    index = np.arange(1, points + 1, dtype=np.int64)
    product = index[:, None] * index[None, :] % (2 * (points + 1))
    table = np.sin(product.astype(np.float64) * (math.pi / (points + 1)))
    high = table.astype(np.float32).astype(ml_dtypes.bfloat16)
    low = (table - high.astype(np.float64)).astype(np.float32).astype(ml_dtypes.bfloat16)
    return high, low


def split(value):
    high = value.astype(BF16)
    low = (value - high.astype(F32)).astype(BF16)
    return high, low


def dot3(value, high_table, low_table):
    high, low = split(value)
    out = jnp.dot(high, high_table, preferred_element_type=F32)
    out += jnp.dot(low, high_table, preferred_element_type=F32)
    return out + jnp.dot(high, low_table, preferred_element_type=F32)


def kernel(
    sizes,
    hist_stat, hist_spec, sine_high_hbm, sine_low_hbm,
    rows_stat, rows_spec, newest_stat, newest_spec,
    sine_high, sine_low, keep, stream, gathered, swap, columns, acc_a, acc_bc, first_cols,
    table_sem, col_sem, keep_sem, stream_sem, swap_send, swap_recv, send_sem, recv_sem,
):
    z_count, m_count, c_count, rows, times, width, kept = sizes
    points = m_count * width
    groups = z_count * c_count
    streamed = rows - kept
    z, m, c = lax.axis_index("hist"), lax.axis_index("mom"), lax.axis_index("rep")
    me = z * c_count + c
    last = groups - 1
    chunks = ((0, rows), (rows, rows + 2 * TILE))
    near = jnp.minimum(z, z_count - 1 - z)

    def source(n):
        paired = n <= 2 * near
        step = jnp.where(paired, (n + 1) // 2, n - near)
        below = jnp.where(paired, n % 2 == 1, 2 * z > z_count - 1)
        return jnp.where(below, z - step, z + step), below

    def group_of(q):
        return source(q // c_count)[0] * c_count + (c + q % c_count) % c_count

    tables = [
        pltpu.make_async_copy(sine_high_hbm, sine_high, table_sem.at[0]),
        pltpu.make_async_copy(sine_low_hbm, sine_low, table_sem.at[1]),
    ]
    cols = [
        pltpu.make_async_copy(h.at[:, pl.ds(times - TILE, TILE), :], first_cols.at[k], col_sem.at[k])
        for k, h in enumerate((hist_stat, hist_spec))
    ]
    for copy in cols + tables:
        copy.start()

    def keep_copies(q):
        part = pl.ds(pl.multiple_of(group_of(q) * rows, TILE), rows)
        return [
            pltpu.make_async_copy(
                h.at[pl.ds(0, kept), part, :], keep.at[k, :, part, :], keep_sem.at[q, k]
            )
            for k, h in enumerate((hist_stat, hist_spec))
        ]

    def stream_copies(total):
        part = pl.ds(pl.multiple_of(group_of(total % groups) * rows, TILE), rows)
        slot = total % SLOTS
        return [
            pltpu.make_async_copy(
                h.at[pl.ds(kept, streamed), part, :], stream.at[slot, k], stream_sem.at[slot, k]
            )
            for k, h in enumerate((hist_stat, hist_spec))
        ]

    barrier = pltpu.get_barrier_semaphore()
    for k in range(1, m_count):
        pl.semaphore_signal(barrier, inc=1, device_id={"mom": (m + k) % m_count}, device_id_type=MESH)
    for k in range(1, c_count):
        pl.semaphore_signal(barrier, inc=1, device_id={"rep": (c + k) % c_count}, device_id_type=MESH)

    @pl.when(z > 0)
    def _():
        pl.semaphore_signal(barrier, inc=1, device_id={"hist": z - 1}, device_id_type=MESH)

    @pl.when(z < z_count - 1)
    def _():
        pl.semaphore_signal(barrier, inc=1, device_id={"hist": z + 1}, device_id_type=MESH)

    for copy in cols:
        copy.wait()

    @pl.loop(0, groups)
    def _(q):
        for copy in keep_copies(q):
            copy.start()
        if streamed:
            @pl.when(q < SLOTS)
            def _():
                for copy in stream_copies(q):
                    copy.start()

    columns[0, 0] = first_cols[0, :, TILE - 2, :]
    columns[0, 1] = first_cols[0, :, TILE - 1, :]
    columns[1, 0] = -first_cols[1, :, TILE - 2, :]
    columns[1, 1] = -first_cols[1, :, TILE - 1, :]
    outs = (rows_stat, rows_spec)

    def column(k, a):
        return columns[k, a] if a < 2 else outs[k][a - 2]

    along = jnp.where(z > 0, 1, 0) + jnp.where(z < z_count - 1, 1, 0)
    pl.semaphore_wait(barrier, m_count - 1 + c_count - 1 + along)

    dp = CUTOFF / points
    dr = math.pi / ((points + 1) * dp)
    every = lax.broadcasted_iota(jnp.int32, (1, points), 1).astype(F32) + 1.0
    radius = every * dr
    inverse_radius = 1.0 / radius
    back_factor = (4.0 * math.pi * dr) * radius
    lane = lax.broadcasted_iota(jnp.int32, (1, width), 1)
    momentum = ((lane + m * width).astype(F32) + 1.0) * dp
    inverse_momentum = 1.0 / momentum

    def momenta_of(part):
        return ((lane + part * width).astype(F32) + 1.0) * dp

    row_time = me * rows + lax.broadcasted_iota(jnp.int32, (rows, 1), 0)
    is_last = (me == last).astype(F32)
    factor = TIME_STEP * TIME_STEP
    extended = rows + TILE
    own_part = pl.ds(pl.multiple_of(m * width, LANES), width)
    zero_row = jnp.zeros((1, width), F32)
    block_stat, block_spec = {}, {}
    inner = lax.broadcasted_iota(jnp.int32, (rows, LANES), 0)

    def fold(value):
        return jnp.sum(value.reshape(rows // TILE, TILE, LANES), axis=0)

    def send(s, group, chunk, way, target):
        start, size = chunks[chunk]
        view = gathered.at[s, group, pl.ds(start, size), :]
        return pltpu.make_async_remote_copy(
            src_ref=view,
            dst_ref=view,
            send_sem=send_sem.at[group, chunk, way],
            recv_sem=recv_sem.at[s, group, chunk],
            device_id=target,
            device_id_type=MESH,
        )

    for s in range(STEPS):
        current = s + 1
        for k in range(2):
            blocks = (block_stat, block_spec)[k]
            swap[s, m, k, pl.ds(0, rows), :] = column(k, current)
            extra = [
                blocks[(current, a)] if 2 <= a <= current else zero_row for a in range(TILE)
            ]
            swap[s, m, k, pl.ds(rows, TILE), :] = jnp.concatenate(extra, axis=0)
        swaps = []
        for k in range(1, m_count):
            to = (m + k) % m_count
            copy = pltpu.make_async_remote_copy(
                src_ref=swap.at[s, m],
                dst_ref=swap.at[s, m],
                send_sem=swap_send.at[s, k],
                recv_sem=swap_recv.at[s, k],
                device_id={"mom": to},
                device_id_type=MESH,
            )
            copy.start()
            swaps.append(copy)
        if s == 0:
            for copy in tables:
                copy.wait()

        tadpole_row = rows - 1 if s == 0 else rows + current
        radial = None
        tadpole = None
        for k in range(m_count):
            part = (m - k + m_count) % m_count
            if k:
                swaps[k - 1].wait_recv()
            momenta = momenta_of(part)
            weight = momenta * (dp / (2.0 * math.pi**2))
            value = swap[s, part].reshape(2 * extended, width)
            span = pl.ds(pl.multiple_of(part * width, LANES), width)
            term = dot3(value * weight, sine_high[span, :], sine_low[span, :])
            radial = term if radial is None else radial + term
            line = swap[s, part, 0, pl.ds(tadpole_row, 1), :]
            term = jnp.sum(weight * momenta * line, axis=1, keepdims=True)
            tadpole = term if tadpole is None else tadpole + term
        field_stat = radial[:extended] * inverse_radius
        field_spec = radial[extended:] * inverse_radius
        square_stat, square_spec = field_stat * field_stat, field_spec * field_spec
        sigma_stat = -SUNSET_COUPLING * field_stat * (square_stat - 0.75 * square_spec)
        sigma_spec = -SUNSET_COUPLING * field_spec * (3.0 * square_stat - 0.25 * square_spec)
        sigma = jnp.concatenate([sigma_stat * back_factor, sigma_spec * back_factor], axis=0)
        sigma = dot3(sigma, sine_high[:, own_part], sine_low[:, own_part]) * inverse_momentum
        group_stat, group_spec = sigma[:rows], sigma[extended : extended + rows]
        new_stat, new_spec = sigma[rows:extended], sigma[extended + rows :]

        gathered[s, me, pl.ds(0, rows), :] = group_stat
        extra = []
        for a in range(5):
            if a > current:
                extra.append(zero_row)
                continue
            spec = column(1, a)
            if a < 2:
                spec = jnp.where(row_time <= times - 2 + a, spec, 0.0)
            value = group_spec * column(0, a) + group_stat * spec
            extra.append(-jnp.sum(value, axis=0, keepdims=True))
        for a in range(2):
            spec = jnp.where(row_time >= times - 2 + a, column(1, a), 0.0)
            extra.append(jnp.sum(group_spec * spec, axis=0, keepdims=True))
        extra.append(jnp.broadcast_to(tadpole * is_last, (1, width)))
        for k in range(2):
            for b in range(2):
                for a in range(2):
                    corner = columns[k, a, pl.ds(rows - 2 + b, 1), :]
                    extra.append((is_last if k == 0 else -is_last) * corner)
        gathered[s, me, pl.ds(rows, rows + 2 * TILE), :] = jnp.concatenate([group_spec] + extra, axis=0)
        for chunk in range(2):
            @pl.when(z > 0)
            def _():
                send(s, me, chunk, 0, {"hist": z - 1}).start()

            @pl.when(z < z_count - 1)
            def _():
                send(s, me, chunk, 1, {"hist": z + 1}).start()

            for k in range(1, c_count):
                send(s, me, chunk, 1 + k, {"rep": (c + k) % c_count}).start()

        def add_block(q, first):
            group = group_of(q)
            total = s * groups + q
            part = pl.ds(pl.multiple_of(group * rows, TILE), rows)
            if s == 0:
                for copy in keep_copies(q):
                    copy.wait()
            if streamed:
                for copy in stream_copies(total):
                    copy.wait()
            earlier = group < me
            target = jnp.where(earlier, 0, 1)
            for t in range(width // LANES):
                lanes = pl.ds(t * LANES, LANES)
                sig_stat = gathered[s, group, pl.ds(0, rows), lanes]
                sig_spec = gathered[s, group, pl.ds(rows, rows), lanes]
                mixed = sig_spec if first else jnp.where(earlier, sig_stat, sig_spec)

                def body(i, f, r):
                    a = fold(sig_spec * f)
                    if first:
                        acc_a[i, :, lanes] = a
                        acc_bc[0, i, :, lanes] = fold(jnp.where(inner < i, sig_stat, 0.0) * r)
                        acc_bc[1, i, :, lanes] = fold(jnp.where(inner > i, sig_spec, 0.0) * r)
                    else:
                        acc_a[i, :, lanes] += a
                        acc_bc[target, i, :, lanes] += fold(mixed * r)

                @pl.loop(0, kept // ROWS_AT_ONCE)
                def _(b):
                    for u in range(ROWS_AT_ONCE):
                        i = b * ROWS_AT_ONCE + u
                        body(i, keep[0, i, part, lanes], keep[1, i, part, lanes])

                if streamed:
                    slot = total % SLOTS

                    @pl.loop(0, streamed // ROWS_AT_ONCE)
                    def _(b):
                        for u in range(ROWS_AT_ONCE):
                            i = b * ROWS_AT_ONCE + u
                            body(kept + i, stream[slot, 0, i, :, lanes], stream[slot, 1, i, :, lanes])

            if streamed:
                @pl.when(total + SLOTS < STEPS * groups)
                def _():
                    for copy in stream_copies(total + SLOTS):
                        copy.start()

        def from_others(n):
            zz, below = source(n)
            for k in range(1, c_count):
                group = zz * c_count + (c - k + c_count) % c_count
                for chunk in range(2):
                    send(s, group, chunk, 1 + k, {"rep": (c + k) % c_count}).wait_recv()

        add_block(0, True)
        from_others(0)
        for j in range(1, c_count):
            add_block(j, False)

        @pl.loop(1, z_count)
        def _(n):
            zz, below = source(n)
            group = zz * c_count + c
            for chunk in range(2):
                send(s, group, chunk, 0, {"hist": z}).wait_recv()

                @pl.when(below & (z < z_count - 1))
                def _():
                    send(s, group, chunk, 1, {"hist": z + 1}).start()

                @pl.when(jnp.logical_not(below) & (z > 0))
                def _():
                    send(s, group, chunk, 0, {"hist": z - 1}).start()

                for k in range(1, c_count):
                    send(s, group, chunk, 1 + k, {"rep": (c + k) % c_count}).start()
            add_block(n * c_count, False)
            from_others(n)
            for j in range(1, c_count):
                add_block(n * c_count + j, False)

        total = jnp.sum(gathered[s, :, pl.ds(2 * rows, 2 * TILE), :], axis=0)

        def total_row(i):
            return total[i : i + 1]

        if s == 0:
            for b in range(2):
                for a in range(2):
                    block_stat[(b, a)] = total_row(8 + 2 * b + a)
                    block_spec[(b, a)] = total_row(12 + 2 * b + a)
        frequency = momentum * momentum + MASS_SQUARED + HARTREE_COUPLING * total_row(7)

        memory_stat = -(jnp.sum(acc_a[...], axis=1) + jnp.sum(acc_bc[0], axis=1))
        memory_spec = jnp.sum(acc_bc[1], axis=1)
        for b in range(2, current + 1):
            weight = new_spec[b : b + 1]
            memory_stat = memory_stat - weight * column(0, b)
            memory_spec = memory_spec - weight * column(1, b)
        for k, memory in enumerate((memory_stat, memory_spec)):
            now = column(k, current)
            outs[k][s] = 2.0 * now - column(k, s) - factor * (frequency * now + TIME_STEP * memory)

        line_stat, line_spec = [], []
        for a in range(current + 1):
            m_stat = total_row(a)
            m_spec = total_row(5 + a) if a < 2 else zero_row
            for b in range(2, current + 1):
                m_stat = m_stat - new_spec[b : b + 1] * block_stat[(b, a)]
                if b <= a:
                    m_stat = m_stat + new_stat[b : b + 1] * block_spec[(b, a)]
                if b >= a:
                    m_spec = m_spec - new_spec[b : b + 1] * block_spec[(b, a)]
            now = block_stat[(current, a)]
            line_stat.append(
                2.0 * now - block_stat[(s, a)] - factor * (frequency * now + TIME_STEP * m_stat)
            )
            now = block_spec[(current, a)]
            line_spec.append(
                2.0 * now - block_spec[(s, a)] - factor * (frequency * now + TIME_STEP * m_spec)
            )
            newest_memory = m_stat
        line_stat.append(
            2.0 * line_stat[current]
            - line_stat[s]
            - factor * (frequency * line_stat[current] + TIME_STEP * newest_memory)
        )
        line_spec.append(zero_row)
        for a in range(current + 2):
            block_stat[(a, current + 1)] = line_stat[a]
            block_stat[(current + 1, a)] = line_stat[a]
            block_spec[(a, current + 1)] = -line_spec[a]
            block_spec[(current + 1, a)] = line_spec[a]

        for copy in swaps:
            copy.wait_send()

        @pl.loop(0, z_count)
        def _(n):
            zz, below = source(n)
            group = zz * c_count + c
            for chunk in range(2):
                @pl.when(((n == 0) | below) & (z < z_count - 1))
                def _():
                    send(s, group, chunk, 1, {"hist": z + 1}).wait_send()

                @pl.when(((n == 0) | jnp.logical_not(below)) & (z > 0))
                def _():
                    send(s, group, chunk, 0, {"hist": z - 1}).wait_send()

                for k in range(1, c_count):
                    send(s, group, chunk, 1 + k, {"rep": (c + k) % c_count}).wait_send()

    for a in range(STEPS + 2):
        for b in range(STEPS + 2):
            newest_stat[a, pl.ds(b, 1), :] = block_stat[(a, b)]
            newest_spec[a, pl.ds(b, 1), :] = block_spec[(a, b)]


def shards(history_stat, history_spec):
    rows, times, width = history_stat.shape
    z_count, m_count, c_count = (lax.axis_size(a) for a in ("hist", "mom", "rep"))
    groups = z_count * c_count
    points = m_count * width
    newest = STEPS + 2
    row_bytes = 2 * times * width * 4
    kept = min(rows, RESIDENT_BYTES // row_bytes // TILE * TILE)
    streamed = rows - kept
    high, low = sine_table(points)
    sizes = (z_count, m_count, c_count, rows, times, width, kept)
    any_spec = pl.BlockSpec(memory_space=pl.ANY)
    vmem = pl.BlockSpec(memory_space=pltpu.VMEM)
    dma = pltpu.SemaphoreType.DMA
    stream_rows = max(streamed, TILE)
    stream_cols = rows if streamed else TILE
    return pl.pallas_call(
        functools.partial(kernel, sizes),
        out_shape=(
            jax.ShapeDtypeStruct((STEPS, rows, width), F32),
            jax.ShapeDtypeStruct((STEPS, rows, width), F32),
            jax.ShapeDtypeStruct((newest, newest, width), F32),
            jax.ShapeDtypeStruct((newest, newest, width), F32),
        ),
        in_specs=[any_spec] * 4,
        out_specs=(vmem,) * 4,
        scratch_shapes=[
            pltpu.VMEM((points, points), BF16),
            pltpu.VMEM((points, points), BF16),
            pltpu.VMEM((2, kept, times, width), F32),
            pltpu.VMEM((SLOTS, 2, stream_rows, stream_cols, width), F32),
            pltpu.VMEM((STEPS, groups, 2 * rows + 2 * TILE, width), F32),
            pltpu.VMEM((STEPS, m_count, 2, rows + TILE, width), F32),
            pltpu.VMEM((2, 2, rows, width), F32),
            pltpu.VMEM((rows, TILE, width), F32),
            pltpu.VMEM((2, rows, TILE, width), F32),
            pltpu.VMEM((2, rows, TILE, width), F32),
            dma((2,)),
            dma((2,)),
            dma((groups, 2)),
            dma((SLOTS, 2)),
            dma((STEPS, m_count)),
            dma((STEPS, m_count)),
            dma((groups, 2, 1 + c_count)),
            dma((STEPS, groups, 2)),
        ],
        compiler_params=pltpu.CompilerParams(
            collective_id=0, has_side_effects=True, vmem_limit_bytes=67043328
        ),
        name="steps",
    )(history_stat, history_spec, jnp.asarray(high), jnp.asarray(low))


def solution(mesh):
    in_specs = (P(("hist", "rep"), "ens", "mom"), P(("hist", "rep"), "ens", "mom"))
    out_specs = (
        P("ens", ("hist", "rep"), "mom"),
        P("ens", ("hist", "rep"), "mom"),
        P("ens", None, "mom"),
        P("ens", None, "mom"),
    )
    return jax.shard_map(shards, mesh=mesh, in_specs=in_specs, out_specs=out_specs, check_vma=False)
```

```python
import functools
import math

import jax
import jax.numpy as jnp
import ml_dtypes
import numpy as np
from jax import lax
from jax.experimental import pallas as pl
from jax.experimental.pallas import tpu as pltpu
from jax.sharding import PartitionSpec as P

STEPS = 3
TIME_STEP = 0.12
CUTOFF = 12.8
MASS_SQUARED = 1.0
SUNSET_COUPLING = 100.0
HARTREE_COUPLING = 2.45
MESH = pl.DeviceIdType.MESH
LANES = 128
TILE = 8
ROWS_AT_ONCE = 4
SLOTS = 3
RESIDENT_BYTES = 48 << 20
F32 = jnp.float32
BF16 = jnp.bfloat16


def sine_table(points):
    index = np.arange(1, points + 1, dtype=np.int64)
    product = index[:, None] * index[None, :] % (2 * (points + 1))
    table = np.sin(product.astype(np.float64) * (math.pi / (points + 1)))
    high = table.astype(np.float32).astype(ml_dtypes.bfloat16)
    low = (table - high.astype(np.float64)).astype(np.float32).astype(ml_dtypes.bfloat16)
    return high, low


def split(value):
    high = value.astype(BF16)
    low = (value - high.astype(F32)).astype(BF16)
    return high, low


def dot3(value, high_table, low_table):
    high, low = split(value)
    out = jnp.dot(high, high_table, preferred_element_type=F32)
    out += jnp.dot(low, high_table, preferred_element_type=F32)
    return out + jnp.dot(high, low_table, preferred_element_type=F32)


def kernel(
    sizes,
    hist_stat, hist_spec, sine_high_hbm, sine_low_hbm,
    rows_stat, rows_spec, newest_stat, newest_spec,
    sine_high, sine_low, keep, stream, gathered, swap, columns, acc_a, acc_bc, first_cols,
    table_sem, col_sem, keep_sem, stream_sem, swap_send, swap_recv, send_sem, recv_sem,
):
    z_count, m_count, c_count, rows, times, width, kept = sizes
    points = m_count * width
    groups = z_count * c_count
    streamed = rows - kept
    z, m, c = lax.axis_index("hist"), lax.axis_index("mom"), lax.axis_index("rep")
    me = z * c_count + c
    last = groups - 1
    half = rows // 2
    near = jnp.minimum(z, z_count - 1 - z)

    def source(n):
        paired = n <= 2 * near
        step = jnp.where(paired, (n + 1) // 2, n - near)
        below = jnp.where(paired, n % 2 == 1, 2 * z > z_count - 1)
        return jnp.where(below, z - step, z + step), below

    def group_of(q):
        return source(q // c_count)[0] * c_count + (c + q % c_count) % c_count

    tables = [
        pltpu.make_async_copy(sine_high_hbm, sine_high, table_sem.at[0]),
        pltpu.make_async_copy(sine_low_hbm, sine_low, table_sem.at[1]),
    ]
    cols = [
        pltpu.make_async_copy(h.at[:, pl.ds(times - TILE, TILE), :], first_cols.at[k], col_sem.at[k])
        for k, h in enumerate((hist_stat, hist_spec))
    ]
    for copy in cols + tables:
        copy.start()

    def keep_copies(q):
        part = pl.ds(pl.multiple_of(group_of(q) * rows, TILE), rows)
        return [
            pltpu.make_async_copy(
                h.at[pl.ds(0, kept), part, :], keep.at[k, :, part, :], keep_sem.at[q, k]
            )
            for k, h in enumerate((hist_stat, hist_spec))
        ]

    def stream_copies(total):
        part = pl.ds(pl.multiple_of(group_of(total % groups) * rows, TILE), rows)
        slot = total % SLOTS
        return [
            pltpu.make_async_copy(
                h.at[pl.ds(kept, streamed), part, :], stream.at[slot, k], stream_sem.at[slot, k]
            )
            for k, h in enumerate((hist_stat, hist_spec))
        ]

    barrier = pltpu.get_barrier_semaphore()
    for k in range(1, m_count):
        pl.semaphore_signal(barrier, inc=1, device_id={"mom": (m + k) % m_count}, device_id_type=MESH)
    for k in range(1, c_count):
        pl.semaphore_signal(barrier, inc=1, device_id={"rep": (c + k) % c_count}, device_id_type=MESH)

    @pl.when(z > 0)
    def _():
        pl.semaphore_signal(barrier, inc=1, device_id={"hist": z - 1}, device_id_type=MESH)

    @pl.when(z < z_count - 1)
    def _():
        pl.semaphore_signal(barrier, inc=1, device_id={"hist": z + 1}, device_id_type=MESH)

    @pl.loop(0, groups)
    def _(q):
        for copy in keep_copies(q):
            copy.start()
        if streamed:
            @pl.when(q < SLOTS)
            def _():
                for copy in stream_copies(q):
                    copy.start()

    for copy in cols:
        copy.wait()
    columns[0, 0] = first_cols[0, :, TILE - 2, :]
    columns[0, 1] = first_cols[0, :, TILE - 1, :]
    columns[1, 0] = -first_cols[1, :, TILE - 2, :]
    columns[1, 1] = -first_cols[1, :, TILE - 1, :]
    outs = (rows_stat, rows_spec)

    def column(k, a):
        return columns[k, a] if a < 2 else outs[k][a - 2]

    along = jnp.where(z > 0, 1, 0) + jnp.where(z < z_count - 1, 1, 0)
    pl.semaphore_wait(barrier, m_count - 1 + c_count - 1 + along)

    dp = CUTOFF / points
    dr = math.pi / ((points + 1) * dp)
    every = lax.broadcasted_iota(jnp.int32, (1, points), 1).astype(F32) + 1.0
    radius = every * dr
    inverse_radius = 1.0 / radius
    back_factor = (4.0 * math.pi * dr) * radius
    lane = lax.broadcasted_iota(jnp.int32, (1, width), 1)
    momentum = ((lane + m * width).astype(F32) + 1.0) * dp
    inverse_momentum = 1.0 / momentum

    def momenta_of(part):
        return ((lane + part * width).astype(F32) + 1.0) * dp

    row_time = me * rows + lax.broadcasted_iota(jnp.int32, (rows, 1), 0)
    is_last = (me == last).astype(F32)
    factor = TIME_STEP * TIME_STEP
    extended = rows + TILE
    own_part = pl.ds(pl.multiple_of(m * width, LANES), width)
    zero_row = jnp.zeros((1, width), F32)
    block_stat, block_spec = {}, {}
    inner = lax.broadcasted_iota(jnp.int32, (rows, LANES), 0)

    def fold(value):
        return jnp.sum(value.reshape(rows // TILE, TILE, LANES), axis=0)

    def send(s, group, chunk, way, target):
        start = chunk * rows
        size = rows + (0 if chunk == 0 else 2 * TILE if s == 0 else TILE)
        view = gathered.at[s, group, pl.ds(start, size), :]
        return pltpu.make_async_remote_copy(
            src_ref=view,
            dst_ref=view,
            send_sem=send_sem.at[group, chunk, way],
            recv_sem=recv_sem.at[s, group, chunk],
            device_id=target,
            device_id_type=MESH,
        )

    def drain(s):
        @pl.loop(0, z_count)
        def _(n):
            zz, below = source(n)
            group = zz * c_count + c
            for chunk in range(2):
                @pl.when(((n == 0) | below) & (z < z_count - 1))
                def _():
                    send(s, group, chunk, 1, {"hist": z + 1}).wait_send()

                @pl.when(((n == 0) | jnp.logical_not(below)) & (z > 0))
                def _():
                    send(s, group, chunk, 0, {"hist": z - 1}).wait_send()

                for k in range(1, c_count):
                    send(s, group, chunk, 1 + k, {"rep": (c + k) % c_count}).wait_send()

    for s in range(STEPS):
        current = s + 1
        for k in range(2):
            blocks = (block_stat, block_spec)[k]
            swap[s, m, k, pl.ds(0, rows), :] = column(k, current)
            extra = [
                blocks[(current, a)] if 2 <= a <= current else zero_row for a in range(TILE)
            ]
            swap[s, m, k, pl.ds(rows, TILE), :] = jnp.concatenate(extra, axis=0)
        pieces = ((0, half), (half, half + TILE))
        swaps = []
        for start, size in pieces:
            for k in range(1, m_count):
                view = swap.at[s, m, :, pl.ds(start, size), :]
                copy = pltpu.make_async_remote_copy(
                    src_ref=view,
                    dst_ref=view,
                    send_sem=swap_send.at[s, len(swaps)],
                    recv_sem=swap_recv.at[s, len(swaps)],
                    device_id={"mom": (m + k) % m_count},
                    device_id_type=MESH,
                )
                copy.start()
                swaps.append(copy)
        if s == 0:
            for copy in tables:
                copy.wait()

        tadpole_row = rows - 1 if s == 0 else rows + current
        halves = []
        for piece, (start, size) in enumerate(pieces):
            radial = None
            tadpole = None
            for k in range(m_count):
                part = (m - k + m_count) % m_count
                if k:
                    swaps[piece * (m_count - 1) + k - 1].wait_recv()
                momenta = momenta_of(part)
                weight = momenta * (dp / (2.0 * math.pi**2))
                value = swap[s, part, :, pl.ds(start, size), :].reshape(2 * size, width)
                span = pl.ds(pl.multiple_of(part * width, LANES), width)
                term = dot3(value * weight, sine_high[span, :], sine_low[span, :])
                radial = term if radial is None else radial + term
                if piece:
                    line = swap[s, part, 0, pl.ds(tadpole_row, 1), :]
                    term = jnp.sum(weight * momenta * line, axis=1, keepdims=True)
                    tadpole = term if tadpole is None else tadpole + term
            field_stat = radial[:size] * inverse_radius
            field_spec = radial[size:] * inverse_radius
            square_stat, square_spec = field_stat * field_stat, field_spec * field_spec
            sigma_stat = -SUNSET_COUPLING * field_stat * (square_stat - 0.75 * square_spec)
            sigma_spec = -SUNSET_COUPLING * field_spec * (3.0 * square_stat - 0.25 * square_spec)
            sigma = jnp.concatenate([sigma_stat * back_factor, sigma_spec * back_factor], axis=0)
            sigma = dot3(sigma, sine_high[:, own_part], sine_low[:, own_part]) * inverse_momentum
            halves.append((sigma[:half], sigma[size : size + half]))
            if piece == 0:
                gathered[s, me, pl.ds(0, rows), :] = jnp.concatenate(halves[0], axis=0)
                if s:
                    drain(s - 1)
            else:
                group_stat = jnp.concatenate([halves[0][0], halves[1][0]], axis=0)
                group_spec = jnp.concatenate([halves[0][1], halves[1][1]], axis=0)
                new_stat, new_spec = sigma[half:size], sigma[size + half :]
                extra = []
                for a in range(5):
                    if a > current:
                        extra.append(zero_row)
                        continue
                    spec = column(1, a)
                    if a < 2:
                        spec = jnp.where(row_time <= times - 2 + a, spec, 0.0)
                    value = group_spec * column(0, a) + group_stat * spec
                    extra.append(-jnp.sum(value, axis=0, keepdims=True))
                for a in range(2):
                    spec = jnp.where(row_time >= times - 2 + a, column(1, a), 0.0)
                    extra.append(jnp.sum(group_spec * spec, axis=0, keepdims=True))
                extra.append(jnp.broadcast_to(tadpole * is_last, (1, width)))
                if s == 0:
                    for k in range(2):
                        for b in range(2):
                            for a in range(2):
                                corner = columns[k, a, pl.ds(rows - 2 + b, 1), :]
                                extra.append((is_last if k == 0 else -is_last) * corner)
                gathered[s, me, pl.ds(rows, rows + len(extra)), :] = jnp.concatenate(
                    list(halves[1]) + extra, axis=0
                )

            @pl.when(z > 0)
            def _():
                send(s, me, piece, 0, {"hist": z - 1}).start()

            @pl.when(z < z_count - 1)
            def _():
                send(s, me, piece, 1, {"hist": z + 1}).start()

            for k in range(1, c_count):
                send(s, me, piece, 1 + k, {"rep": (c + k) % c_count}).start()

        def add_block(q, first):
            group = group_of(q)
            total = s * groups + q
            part = pl.ds(pl.multiple_of(group * rows, TILE), rows)
            if s == 0:
                for copy in keep_copies(q):
                    copy.wait()
            if streamed:
                for copy in stream_copies(total):
                    copy.wait()
            earlier = group < me
            target = jnp.where(earlier, 0, 1)
            for t in range(width // LANES):
                lanes = pl.ds(t * LANES, LANES)
                parts = [gathered[s, group, pl.ds(u * half, half), lanes] for u in range(4)]
                sig_stat = jnp.concatenate([parts[0], parts[2]], axis=0)
                sig_spec = jnp.concatenate([parts[1], parts[3]], axis=0)
                mixed = sig_spec if first else jnp.where(earlier, sig_stat, sig_spec)

                def body(i, f, r):
                    a = fold(sig_spec * f)
                    if first:
                        acc_a[i, :, lanes] = a
                        acc_bc[0, i, :, lanes] = fold(jnp.where(inner < i, sig_stat, 0.0) * r)
                        acc_bc[1, i, :, lanes] = fold(jnp.where(inner > i, sig_spec, 0.0) * r)
                    else:
                        acc_a[i, :, lanes] += a
                        acc_bc[target, i, :, lanes] += fold(mixed * r)

                @pl.loop(0, kept // ROWS_AT_ONCE)
                def _(b):
                    for u in range(ROWS_AT_ONCE):
                        i = b * ROWS_AT_ONCE + u
                        body(i, keep[0, i, part, lanes], keep[1, i, part, lanes])

                if streamed:
                    slot = total % SLOTS

                    @pl.loop(0, streamed // ROWS_AT_ONCE)
                    def _(b):
                        for u in range(ROWS_AT_ONCE):
                            i = b * ROWS_AT_ONCE + u
                            body(kept + i, stream[slot, 0, i, :, lanes], stream[slot, 1, i, :, lanes])

            if streamed:
                @pl.when(total + SLOTS < STEPS * groups)
                def _():
                    for copy in stream_copies(total + SLOTS):
                        copy.start()

        def from_others(n):
            zz, below = source(n)
            for k in range(1, c_count):
                group = zz * c_count + (c - k + c_count) % c_count
                for chunk in range(2):
                    send(s, group, chunk, 1 + k, {"rep": (c + k) % c_count}).wait_recv()

        def forward(n):
            zz, below = source(n)
            group = zz * c_count + c
            for chunk in range(2):
                send(s, group, chunk, 0, {"hist": z}).wait_recv()

                @pl.when(below & (z < z_count - 1))
                def _():
                    send(s, group, chunk, 1, {"hist": z + 1}).start()

                @pl.when(jnp.logical_not(below) & (z > 0))
                def _():
                    send(s, group, chunk, 0, {"hist": z - 1}).start()

                for k in range(1, c_count):
                    send(s, group, chunk, 1 + k, {"rep": (c + k) % c_count}).start()

        def process(n, first):
            add_block(n * c_count, first)
            from_others(n)
            for j in range(1, c_count):
                add_block(n * c_count + j, False)

        if s == 0:
            @pl.loop(1, z_count)
            def _(n):
                forward(n)

            process(0, True)

            @pl.loop(1, z_count)
            def _(n):
                process(n, False)
        else:
            process(0, True)

            @pl.loop(1, z_count + 1)
            def _(n):
                @pl.when(n < z_count)
                def _():
                    forward(n)

                @pl.when(n > 1)
                def _():
                    process(n - 1, False)

        total = jnp.sum(gathered[s, :, pl.ds(2 * rows, 2 * TILE if s == 0 else TILE), :], axis=0)

        def total_row(i):
            return total[i : i + 1]

        if s == 0:
            for b in range(2):
                for a in range(2):
                    block_stat[(b, a)] = total_row(8 + 2 * b + a)
                    block_spec[(b, a)] = total_row(12 + 2 * b + a)
        frequency = momentum * momentum + MASS_SQUARED + HARTREE_COUPLING * total_row(7)

        memory_stat = -(jnp.sum(acc_a[...], axis=1) + jnp.sum(acc_bc[0], axis=1))
        memory_spec = jnp.sum(acc_bc[1], axis=1)
        for b in range(2, current + 1):
            weight = new_spec[b : b + 1]
            memory_stat = memory_stat - weight * column(0, b)
            memory_spec = memory_spec - weight * column(1, b)
        for k, memory in enumerate((memory_stat, memory_spec)):
            now = column(k, current)
            outs[k][s] = 2.0 * now - column(k, s) - factor * (frequency * now + TIME_STEP * memory)

        line_stat, line_spec = [], []
        for a in range(current + 1):
            m_stat = total_row(a)
            m_spec = total_row(5 + a) if a < 2 else zero_row
            for b in range(2, current + 1):
                m_stat = m_stat - new_spec[b : b + 1] * block_stat[(b, a)]
                if b <= a:
                    m_stat = m_stat + new_stat[b : b + 1] * block_spec[(b, a)]
                if b >= a:
                    m_spec = m_spec - new_spec[b : b + 1] * block_spec[(b, a)]
            now = block_stat[(current, a)]
            line_stat.append(
                2.0 * now - block_stat[(s, a)] - factor * (frequency * now + TIME_STEP * m_stat)
            )
            now = block_spec[(current, a)]
            line_spec.append(
                2.0 * now - block_spec[(s, a)] - factor * (frequency * now + TIME_STEP * m_spec)
            )
            newest_memory = m_stat
        line_stat.append(
            2.0 * line_stat[current]
            - line_stat[s]
            - factor * (frequency * line_stat[current] + TIME_STEP * newest_memory)
        )
        line_spec.append(zero_row)
        for a in range(current + 2):
            block_stat[(a, current + 1)] = line_stat[a]
            block_stat[(current + 1, a)] = line_stat[a]
            block_spec[(a, current + 1)] = -line_spec[a]
            block_spec[(current + 1, a)] = line_spec[a]

        for copy in swaps:
            copy.wait_send()

    drain(STEPS - 1)
    for a in range(STEPS + 2):
        for b in range(STEPS + 2):
            newest_stat[a, pl.ds(b, 1), :] = block_stat[(a, b)]
            newest_spec[a, pl.ds(b, 1), :] = block_spec[(a, b)]


def pass_on(*refs):
    for source, target in zip(refs[:4], refs[4:]):
        target[...] = source[...]


def shards(history_stat, history_spec):
    rows, times, width = history_stat.shape
    z_count, m_count, c_count = (lax.axis_size(a) for a in ("hist", "mom", "rep"))
    groups = z_count * c_count
    points = m_count * width
    newest = STEPS + 2
    row_bytes = 2 * times * width * 4
    kept = min(rows, RESIDENT_BYTES // row_bytes // TILE * TILE)
    streamed = rows - kept
    high, low = sine_table(points)
    sizes = (z_count, m_count, c_count, rows, times, width, kept)
    any_spec = pl.BlockSpec(memory_space=pl.ANY)
    vmem = pl.BlockSpec(memory_space=pltpu.VMEM)
    dma = pltpu.SemaphoreType.DMA
    stream_rows = max(streamed, TILE)
    stream_cols = rows if streamed else TILE
    results = pl.pallas_call(
        functools.partial(kernel, sizes),
        out_shape=(
            jax.ShapeDtypeStruct((STEPS, rows, width), F32),
            jax.ShapeDtypeStruct((STEPS, rows, width), F32),
            jax.ShapeDtypeStruct((newest, newest, width), F32),
            jax.ShapeDtypeStruct((newest, newest, width), F32),
        ),
        in_specs=[any_spec] * 4,
        out_specs=(vmem,) * 4,
        scratch_shapes=[
            pltpu.VMEM((points, points), BF16),
            pltpu.VMEM((points, points), BF16),
            pltpu.VMEM((2, kept, times, width), F32),
            pltpu.VMEM((SLOTS, 2, stream_rows, stream_cols, width), F32),
            pltpu.VMEM((STEPS, groups, 2 * rows + 2 * TILE, width), F32),
            pltpu.VMEM((STEPS, m_count, 2, rows + TILE, width), F32),
            pltpu.VMEM((2, 2, rows, width), F32),
            pltpu.VMEM((rows, TILE, width), F32),
            pltpu.VMEM((2, rows, TILE, width), F32),
            pltpu.VMEM((2, rows, TILE, width), F32),
            dma((2,)),
            dma((2,)),
            dma((groups, 2)),
            dma((SLOTS, 2)),
            dma((STEPS, 2 * m_count)),
            dma((STEPS, 2 * m_count)),
            dma((groups, 2, 1 + c_count)),
            dma((STEPS, groups, 2)),
        ],
        compiler_params=pltpu.CompilerParams(
            collective_id=0, has_side_effects=True, vmem_limit_bytes=67043328
        ),
        name="steps",
    )(history_stat, history_spec, jnp.asarray(high), jnp.asarray(low))
    return pl.pallas_call(
        pass_on,
        out_shape=tuple(jax.ShapeDtypeStruct(r.shape, r.dtype) for r in results),
        in_specs=[vmem] * 4,
        out_specs=(vmem,) * 4,
        name="pass_on",
    )(*results)


def solution(mesh):
    in_specs = (P(("hist", "rep"), "ens", "mom"), P(("hist", "rep"), "ens", "mom"))
    out_specs = (
        P("ens", ("hist", "rep"), "mom"),
        P("ens", ("hist", "rep"), "mom"),
        P("ens", None, "mom"),
        P("ens", None, "mom"),
    )
    return jax.shard_map(shards, mesh=mesh, in_specs=in_specs, out_specs=out_specs, check_vma=False)
```

```python
import functools
import math

import jax
import jax.numpy as jnp
import ml_dtypes
import numpy as np
from jax import lax
from jax.experimental import pallas as pl
from jax.experimental.pallas import tpu as pltpu
from jax.sharding import PartitionSpec as P

STEPS = 3
TIME_STEP = 0.12
CUTOFF = 12.8
MASS_SQUARED = 1.0
SUNSET_COUPLING = 100.0
HARTREE_COUPLING = 2.45
MESH = pl.DeviceIdType.MESH
LANES = 128
TILE = 8
ROWS_AT_ONCE = 4
SLOTS = 3
RESIDENT_BYTES = 48 << 20
F32 = jnp.float32
BF16 = jnp.bfloat16


def sine_table(points):
    index = np.arange(1, points + 1, dtype=np.int64)
    product = index[:, None] * index[None, :] % (2 * (points + 1))
    table = np.sin(product.astype(np.float64) * (math.pi / (points + 1)))
    high = table.astype(np.float32).astype(ml_dtypes.bfloat16)
    low = (table - high.astype(np.float64)).astype(np.float32).astype(ml_dtypes.bfloat16)
    return high, low


def split(value):
    high = value.astype(BF16)
    low = (value - high.astype(F32)).astype(BF16)
    return high, low


def dot3(value, high_table, low_table):
    high, low = split(value)
    out = jnp.dot(high, high_table, preferred_element_type=F32)
    out += jnp.dot(low, high_table, preferred_element_type=F32)
    return out + jnp.dot(high, low_table, preferred_element_type=F32)


def kernel(
    sizes,
    hist_stat, hist_spec, sine_high_hbm, sine_low_hbm,
    rows_stat, rows_spec, newest_stat, newest_spec,
    sine_high, sine_low, keep, stream, gathered, swap, columns, acc_a, acc_bc, first_cols,
    table_sem, col_sem, keep_sem, stream_sem, swap_send, swap_recv, send_sem, recv_sem,
):
    z_count, m_count, c_count, rows, times, width, kept = sizes
    points = m_count * width
    groups = z_count * c_count
    streamed = rows - kept
    z, m, c = lax.axis_index("hist"), lax.axis_index("mom"), lax.axis_index("rep")
    me = z * c_count + c
    last = groups - 1
    half = rows // 2
    near = jnp.minimum(z, z_count - 1 - z)

    def source(n):
        paired = n <= 2 * near
        step = jnp.where(paired, (n + 1) // 2, n - near)
        below = jnp.where(paired, n % 2 == 1, 2 * z > z_count - 1)
        return jnp.where(below, z - step, z + step), below

    def group_of(q):
        return source(q // c_count)[0] * c_count + (c + q % c_count) % c_count

    tables = [
        pltpu.make_async_copy(sine_high_hbm, sine_high, table_sem.at[0]),
        pltpu.make_async_copy(sine_low_hbm, sine_low, table_sem.at[1]),
    ]
    cols = [
        pltpu.make_async_copy(h.at[:, pl.ds(times - TILE, TILE), :], first_cols.at[k], col_sem.at[k])
        for k, h in enumerate((hist_stat, hist_spec))
    ]
    for copy in cols + tables:
        copy.start()

    def keep_copies(q):
        part = pl.ds(pl.multiple_of(group_of(q) * rows, TILE), rows)
        return [
            pltpu.make_async_copy(
                h.at[pl.ds(0, kept), part, :], keep.at[k, :, part, :], keep_sem.at[q, k]
            )
            for k, h in enumerate((hist_stat, hist_spec))
        ]

    def stream_copies(total):
        part = pl.ds(pl.multiple_of(group_of(total % groups) * rows, TILE), rows)
        slot = total % SLOTS
        return [
            pltpu.make_async_copy(
                h.at[pl.ds(kept, streamed), part, :], stream.at[slot, k], stream_sem.at[slot, k]
            )
            for k, h in enumerate((hist_stat, hist_spec))
        ]

    barrier = pltpu.get_barrier_semaphore()
    for k in range(1, m_count):
        pl.semaphore_signal(barrier, inc=1, device_id={"mom": (m + k) % m_count}, device_id_type=MESH)
    for k in range(1, c_count):
        pl.semaphore_signal(barrier, inc=1, device_id={"rep": (c + k) % c_count}, device_id_type=MESH)

    @pl.when(z > 0)
    def _():
        pl.semaphore_signal(barrier, inc=1, device_id={"hist": z - 1}, device_id_type=MESH)

    @pl.when(z < z_count - 1)
    def _():
        pl.semaphore_signal(barrier, inc=1, device_id={"hist": z + 1}, device_id_type=MESH)

    def start_keep(begin, end):
        @pl.loop(begin, end)
        def _(q):
            for copy in keep_copies(q):
                copy.start()
            if streamed:
                @pl.when(q < SLOTS)
                def _():
                    for copy in stream_copies(q):
                        copy.start()

    first_part, second_part = groups // 2, groups // 2 + groups // 4
    start_keep(0, first_part)
    for copy in cols:
        copy.wait()
    columns[0, 0] = first_cols[0, :, TILE - 2, :]
    columns[0, 1] = first_cols[0, :, TILE - 1, :]
    columns[1, 0] = -first_cols[1, :, TILE - 2, :]
    columns[1, 1] = -first_cols[1, :, TILE - 1, :]
    outs = (rows_stat, rows_spec)

    def column(k, a):
        return columns[k, a] if a < 2 else outs[k][a - 2]

    along = jnp.where(z > 0, 1, 0) + jnp.where(z < z_count - 1, 1, 0)
    pl.semaphore_wait(barrier, m_count - 1 + c_count - 1 + along)

    dp = CUTOFF / points
    dr = math.pi / ((points + 1) * dp)
    every = lax.broadcasted_iota(jnp.int32, (1, points), 1).astype(F32) + 1.0
    radius = every * dr
    inverse_radius = 1.0 / radius
    back_factor = (4.0 * math.pi * dr) * radius
    lane = lax.broadcasted_iota(jnp.int32, (1, width), 1)
    momentum = ((lane + m * width).astype(F32) + 1.0) * dp
    inverse_momentum = 1.0 / momentum

    def momenta_of(part):
        return ((lane + part * width).astype(F32) + 1.0) * dp

    row_time = me * rows + lax.broadcasted_iota(jnp.int32, (rows, 1), 0)
    is_last = (me == last).astype(F32)
    factor = TIME_STEP * TIME_STEP
    extended = rows + TILE
    own_part = pl.ds(pl.multiple_of(m * width, LANES), width)
    zero_row = jnp.zeros((1, width), F32)
    block_stat, block_spec = {}, {}
    inner = lax.broadcasted_iota(jnp.int32, (rows, LANES), 0)

    def fold(value):
        return jnp.sum(value.reshape(rows // TILE, TILE, LANES), axis=0)

    def send(s, group, chunk, way, target):
        start = chunk * rows
        size = rows + (0 if chunk == 0 else 2 * TILE if s == 0 else TILE)
        view = gathered.at[s, group, pl.ds(start, size), :]
        return pltpu.make_async_remote_copy(
            src_ref=view,
            dst_ref=view,
            send_sem=send_sem.at[group, chunk, way],
            recv_sem=recv_sem.at[s, group, chunk],
            device_id=target,
            device_id_type=MESH,
        )

    def drain(s):
        @pl.loop(0, z_count)
        def _(n):
            zz, below = source(n)
            group = zz * c_count + c
            for chunk in range(2):
                @pl.when(((n == 0) | below) & (z < z_count - 1))
                def _():
                    send(s, group, chunk, 1, {"hist": z + 1}).wait_send()

                @pl.when(((n == 0) | jnp.logical_not(below)) & (z > 0))
                def _():
                    send(s, group, chunk, 0, {"hist": z - 1}).wait_send()

                for k in range(1, c_count):
                    send(s, group, chunk, 1 + k, {"rep": (c + k) % c_count}).wait_send()

    for s in range(STEPS):
        current = s + 1
        for k in range(2):
            blocks = (block_stat, block_spec)[k]
            swap[s, m, k, pl.ds(0, rows), :] = column(k, current)
            extra = [
                blocks[(current, a)] if 2 <= a <= current else zero_row for a in range(TILE)
            ]
            swap[s, m, k, pl.ds(rows, TILE), :] = jnp.concatenate(extra, axis=0)
        pieces = ((0, half), (half, half + TILE))
        swaps = []
        for start, size in pieces:
            for k in range(1, m_count):
                view = swap.at[s, m, :, pl.ds(start, size), :]
                copy = pltpu.make_async_remote_copy(
                    src_ref=view,
                    dst_ref=view,
                    send_sem=swap_send.at[s, len(swaps)],
                    recv_sem=swap_recv.at[s, len(swaps)],
                    device_id={"mom": (m + k) % m_count},
                    device_id_type=MESH,
                )
                copy.start()
                swaps.append(copy)
        if s == 0:
            for copy in tables:
                copy.wait()

        tadpole_row = rows - 1 if s == 0 else rows + current
        halves = []
        for piece, (start, size) in enumerate(pieces):
            radial = None
            tadpole = None
            for k in range(m_count):
                part = (m - k + m_count) % m_count
                if k:
                    swaps[piece * (m_count - 1) + k - 1].wait_recv()
                momenta = momenta_of(part)
                weight = momenta * (dp / (2.0 * math.pi**2))
                value = swap[s, part, :, pl.ds(start, size), :].reshape(2 * size, width)
                span = pl.ds(pl.multiple_of(part * width, LANES), width)
                term = dot3(value * weight, sine_high[span, :], sine_low[span, :])
                radial = term if radial is None else radial + term
                if piece:
                    line = swap[s, part, 0, pl.ds(tadpole_row, 1), :]
                    term = jnp.sum(weight * momenta * line, axis=1, keepdims=True)
                    tadpole = term if tadpole is None else tadpole + term
            field_stat = radial[:size] * inverse_radius
            field_spec = radial[size:] * inverse_radius
            square_stat, square_spec = field_stat * field_stat, field_spec * field_spec
            sigma_stat = -SUNSET_COUPLING * field_stat * (square_stat - 0.75 * square_spec)
            sigma_spec = -SUNSET_COUPLING * field_spec * (3.0 * square_stat - 0.25 * square_spec)
            sigma = jnp.concatenate([sigma_stat * back_factor, sigma_spec * back_factor], axis=0)
            sigma = dot3(sigma, sine_high[:, own_part], sine_low[:, own_part]) * inverse_momentum
            halves.append((sigma[:half], sigma[size : size + half]))
            if piece == 0:
                gathered[s, me, pl.ds(0, rows), :] = jnp.concatenate(halves[0], axis=0)
                if s:
                    drain(s - 1)
            else:
                group_stat = jnp.concatenate([halves[0][0], halves[1][0]], axis=0)
                group_spec = jnp.concatenate([halves[0][1], halves[1][1]], axis=0)
                new_stat, new_spec = sigma[half:size], sigma[size + half :]
                extra = []
                for a in range(5):
                    if a > current:
                        extra.append(zero_row)
                        continue
                    spec = column(1, a)
                    if a < 2:
                        spec = jnp.where(row_time <= times - 2 + a, spec, 0.0)
                    value = group_spec * column(0, a) + group_stat * spec
                    extra.append(-jnp.sum(value, axis=0, keepdims=True))
                for a in range(2):
                    spec = jnp.where(row_time >= times - 2 + a, column(1, a), 0.0)
                    extra.append(jnp.sum(group_spec * spec, axis=0, keepdims=True))
                extra.append(jnp.broadcast_to(tadpole * is_last, (1, width)))
                if s == 0:
                    for k in range(2):
                        for b in range(2):
                            for a in range(2):
                                corner = columns[k, a, pl.ds(rows - 2 + b, 1), :]
                                extra.append((is_last if k == 0 else -is_last) * corner)
                gathered[s, me, pl.ds(rows, rows + len(extra)), :] = jnp.concatenate(
                    list(halves[1]) + extra, axis=0
                )

            @pl.when(z > 0)
            def _():
                send(s, me, piece, 0, {"hist": z - 1}).start()

            @pl.when(z < z_count - 1)
            def _():
                send(s, me, piece, 1, {"hist": z + 1}).start()

            for k in range(1, c_count):
                send(s, me, piece, 1 + k, {"rep": (c + k) % c_count}).start()

        def add_block(q, first):
            group = group_of(q)
            total = s * groups + q
            part = pl.ds(pl.multiple_of(group * rows, TILE), rows)
            if s == 0:
                for copy in keep_copies(q):
                    copy.wait()
            if streamed:
                for copy in stream_copies(total):
                    copy.wait()
            earlier = group < me
            target = jnp.where(earlier, 0, 1)
            for t in range(width // LANES):
                lanes = pl.ds(t * LANES, LANES)
                parts = [gathered[s, group, pl.ds(u * half, half), lanes] for u in range(4)]
                sig_stat = jnp.concatenate([parts[0], parts[2]], axis=0)
                sig_spec = jnp.concatenate([parts[1], parts[3]], axis=0)
                mixed = sig_spec if first else jnp.where(earlier, sig_stat, sig_spec)

                def body(i, f, r):
                    a = fold(sig_spec * f)
                    if first:
                        acc_a[i, :, lanes] = a
                        acc_bc[0, i, :, lanes] = fold(jnp.where(inner < i, sig_stat, 0.0) * r)
                        acc_bc[1, i, :, lanes] = fold(jnp.where(inner > i, sig_spec, 0.0) * r)
                    else:
                        acc_a[i, :, lanes] += a
                        acc_bc[target, i, :, lanes] += fold(mixed * r)

                @pl.loop(0, kept // ROWS_AT_ONCE)
                def _(b):
                    for u in range(ROWS_AT_ONCE):
                        i = b * ROWS_AT_ONCE + u
                        body(i, keep[0, i, part, lanes], keep[1, i, part, lanes])

                if streamed:
                    slot = total % SLOTS

                    @pl.loop(0, streamed // ROWS_AT_ONCE)
                    def _(b):
                        for u in range(ROWS_AT_ONCE):
                            i = b * ROWS_AT_ONCE + u
                            body(kept + i, stream[slot, 0, i, :, lanes], stream[slot, 1, i, :, lanes])

            if streamed:
                @pl.when(total + SLOTS < STEPS * groups)
                def _():
                    for copy in stream_copies(total + SLOTS):
                        copy.start()

        def from_others(n):
            zz, below = source(n)
            for k in range(1, c_count):
                group = zz * c_count + (c - k + c_count) % c_count
                for chunk in range(2):
                    send(s, group, chunk, 1 + k, {"rep": (c + k) % c_count}).wait_recv()

        def forward(n):
            zz, below = source(n)
            group = zz * c_count + c
            for chunk in range(2):
                send(s, group, chunk, 0, {"hist": z}).wait_recv()

                @pl.when(below & (z < z_count - 1))
                def _():
                    send(s, group, chunk, 1, {"hist": z + 1}).start()

                @pl.when(jnp.logical_not(below) & (z > 0))
                def _():
                    send(s, group, chunk, 0, {"hist": z - 1}).start()

                for k in range(1, c_count):
                    send(s, group, chunk, 1 + k, {"rep": (c + k) % c_count}).start()

        def process(n, first):
            add_block(n * c_count, first)
            from_others(n)
            for j in range(1, c_count):
                add_block(n * c_count + j, False)

        if s == 0:
            start_keep(first_part, second_part)
            forward(1)
            start_keep(second_part, groups)
        process(0, True)
        lag = jnp.where(near > 0, 1, 0) if s else 1

        @pl.loop(1, z_count + 1)
        def _(n):
            @pl.when((n > (0 if s else 1)) & (n < z_count))
            def _():
                forward(n)

            @pl.when((n - lag > 0) & (n - lag < z_count))
            def _():
                process(n - lag, False)

        total = jnp.sum(gathered[s, :, pl.ds(2 * rows, 2 * TILE if s == 0 else TILE), :], axis=0)

        def total_row(i):
            return total[i : i + 1]

        if s == 0:
            for b in range(2):
                for a in range(2):
                    block_stat[(b, a)] = total_row(8 + 2 * b + a)
                    block_spec[(b, a)] = total_row(12 + 2 * b + a)
        frequency = momentum * momentum + MASS_SQUARED + HARTREE_COUPLING * total_row(7)

        memory_stat = -(jnp.sum(acc_a[...], axis=1) + jnp.sum(acc_bc[0], axis=1))
        memory_spec = jnp.sum(acc_bc[1], axis=1)
        for b in range(2, current + 1):
            weight = new_spec[b : b + 1]
            memory_stat = memory_stat - weight * column(0, b)
            memory_spec = memory_spec - weight * column(1, b)
        for k, memory in enumerate((memory_stat, memory_spec)):
            now = column(k, current)
            outs[k][s] = 2.0 * now - column(k, s) - factor * (frequency * now + TIME_STEP * memory)

        line_stat, line_spec = [], []
        for a in range(current + 1):
            m_stat = total_row(a)
            m_spec = total_row(5 + a) if a < 2 else zero_row
            for b in range(2, current + 1):
                m_stat = m_stat - new_spec[b : b + 1] * block_stat[(b, a)]
                if b <= a:
                    m_stat = m_stat + new_stat[b : b + 1] * block_spec[(b, a)]
                if b >= a:
                    m_spec = m_spec - new_spec[b : b + 1] * block_spec[(b, a)]
            now = block_stat[(current, a)]
            line_stat.append(
                2.0 * now - block_stat[(s, a)] - factor * (frequency * now + TIME_STEP * m_stat)
            )
            now = block_spec[(current, a)]
            line_spec.append(
                2.0 * now - block_spec[(s, a)] - factor * (frequency * now + TIME_STEP * m_spec)
            )
            newest_memory = m_stat
        line_stat.append(
            2.0 * line_stat[current]
            - line_stat[s]
            - factor * (frequency * line_stat[current] + TIME_STEP * newest_memory)
        )
        line_spec.append(zero_row)
        for a in range(current + 2):
            block_stat[(a, current + 1)] = line_stat[a]
            block_stat[(current + 1, a)] = line_stat[a]
            block_spec[(a, current + 1)] = -line_spec[a]
            block_spec[(current + 1, a)] = line_spec[a]

        for copy in swaps:
            copy.wait_send()

    drain(STEPS - 1)
    for a in range(STEPS + 2):
        for b in range(STEPS + 2):
            newest_stat[a, pl.ds(b, 1), :] = block_stat[(a, b)]
            newest_spec[a, pl.ds(b, 1), :] = block_spec[(a, b)]


def pass_on(*refs):
    for source, target in zip(refs[:4], refs[4:]):
        target[...] = source[...]


def shards(history_stat, history_spec):
    rows, times, width = history_stat.shape
    z_count, m_count, c_count = (lax.axis_size(a) for a in ("hist", "mom", "rep"))
    groups = z_count * c_count
    points = m_count * width
    newest = STEPS + 2
    row_bytes = 2 * times * width * 4
    kept = min(rows, RESIDENT_BYTES // row_bytes // TILE * TILE)
    streamed = rows - kept
    high, low = sine_table(points)
    sizes = (z_count, m_count, c_count, rows, times, width, kept)
    any_spec = pl.BlockSpec(memory_space=pl.ANY)
    vmem = pl.BlockSpec(memory_space=pltpu.VMEM)
    dma = pltpu.SemaphoreType.DMA
    stream_rows = max(streamed, TILE)
    stream_cols = rows if streamed else TILE
    results = pl.pallas_call(
        functools.partial(kernel, sizes),
        out_shape=(
            jax.ShapeDtypeStruct((STEPS, rows, width), F32),
            jax.ShapeDtypeStruct((STEPS, rows, width), F32),
            jax.ShapeDtypeStruct((newest, newest, width), F32),
            jax.ShapeDtypeStruct((newest, newest, width), F32),
        ),
        in_specs=[any_spec] * 4,
        out_specs=(vmem,) * 4,
        scratch_shapes=[
            pltpu.VMEM((points, points), BF16),
            pltpu.VMEM((points, points), BF16),
            pltpu.VMEM((2, kept, times, width), F32),
            pltpu.VMEM((SLOTS, 2, stream_rows, stream_cols, width), F32),
            pltpu.VMEM((STEPS, groups, 2 * rows + 2 * TILE, width), F32),
            pltpu.VMEM((STEPS, m_count, 2, rows + TILE, width), F32),
            pltpu.VMEM((2, 2, rows, width), F32),
            pltpu.VMEM((rows, TILE, width), F32),
            pltpu.VMEM((2, rows, TILE, width), F32),
            pltpu.VMEM((2, rows, TILE, width), F32),
            dma((2,)),
            dma((2,)),
            dma((groups, 2)),
            dma((SLOTS, 2)),
            dma((STEPS, 2 * m_count)),
            dma((STEPS, 2 * m_count)),
            dma((groups, 2, 1 + c_count)),
            dma((STEPS, groups, 2)),
        ],
        compiler_params=pltpu.CompilerParams(
            collective_id=0, has_side_effects=True, vmem_limit_bytes=67043328
        ),
        name="steps",
    )(history_stat, history_spec, jnp.asarray(high), jnp.asarray(low))
    return pl.pallas_call(
        pass_on,
        out_shape=tuple(jax.ShapeDtypeStruct(r.shape, r.dtype) for r in results),
        in_specs=[vmem] * 4,
        out_specs=(vmem,) * 4,
        name="pass_on",
    )(*results)


def solution(mesh):
    in_specs = (P(("hist", "rep"), "ens", "mom"), P(("hist", "rep"), "ens", "mom"))
    out_specs = (
        P("ens", ("hist", "rep"), "mom"),
        P("ens", ("hist", "rep"), "mom"),
        P("ens", None, "mom"),
        P("ens", None, "mom"),
    )
    return jax.shard_map(shards, mesh=mesh, in_specs=in_specs, out_specs=out_specs, check_vma=False)
```
